256 devices in a mesh: fsdp: 64 (over z, x_hi, y), tp: 4 (over x_lo, core).
Axes of the slice: x: 4 (x_hi: 2, x_lo: 2; x = x_hi * 2 + x_lo), y: 4, z: 8, core: 2. Of those that a mesh axis runs over, the one named last changes fastest.
Arguments:
- tokens: bfloat16 [24576, 8192], P('fsdp', 'tp'), may hold values from -16 to 16
- cotangent: bfloat16 [24576, 1024], P('fsdp', 'tp'), may hold values from -6 to 6
- response_mask: int32 [24576], P('fsdp'), may hold values 0 or 1
- key_weight: bfloat16 [8192, 1024], P('fsdp', 'tp'), may hold values from -0.0625 to 0.0625
- new_hidden: bfloat16 [256, 8, 8192], P('fsdp'), may hold values from -6 to 6
- new_values: bfloat16 [256, 8, 1024], P('fsdp', None, 'tp'), may hold values from -6 to 6
- queries: bfloat16 [256, 8, 8192], P('fsdp', None, 'tp'), may hold values from -16 to 16, as said below
- cache_keys: bfloat16 [256, 2048, 1024], P('fsdp', None, 'tp'), may hold values from -16 to 16, as said below
- cache_values: bfloat16 [256, 2048, 1024], P('fsdp', None, 'tp'), may hold values from -6 to 6
- cache_lengths: int32 [256], P('fsdp'), may hold values from 1 to 2048, as said below
Outputs:
- grad_inputs: bfloat16 [24576, 8192], P('fsdp', 'tp')
- learner_weight: bfloat16 [8192, 1024], P('fsdp', 'tp')
- new_keys: bfloat16 [256, 8, 1024], P('fsdp', None, 'tp')
- context: bfloat16 [256, 8, 8192], P('fsdp', None, 'tp')
The draws below stay inside these ranges and needn't reach their ends.
Inputs may be any that keep to these rules, and one draw needn't show every extreme that they name: `queries`: queries of the decoded tokens, already rotated. `cache_keys`: cached keys, already rotated. `cache_lengths`: some request has exactly 2048 valid slots.
All inputs are finite; a program needn't handle non-finite values. No bound on the sum of `response_mask` on one device may be relied on, other than what follows from the above.
Results may differ from the reference program's by a relative error of at most 0.0095.
Values may be sent and summed in bfloat16 or wider, within the bound.
No kernel may reach another device: no remote copies, remote signals or barrier semaphores. Data moves between devices by JAX's collectives and lax.ppermute only.
A program may use at most 128 MiB of HBM per device.

```python
import math
import jax
import jax.numpy as jnp
from jax import lax

D = 8192
QH = 64
KVH = 8
HD = 128
CACHE = 2048
STEPS = 8
KVW = 1024
TOKENS = 24576
BATCH = 256
N_TP = 4


def draw_cache_keys(key, part):
    noise = jnp.clip(jax.random.normal(jax.random.fold_in(key, 1), (BATCH, CACHE, KVH * HD), jnp.float32), -6.0, 6.0)
    return noise.astype(jnp.bfloat16)


def draw_queries(key, part):
    noise = jnp.clip(jax.random.normal(jax.random.fold_in(key, 3), (BATCH, STEPS, KVH, QH // KVH, HD), jnp.float32), -6.0, 6.0)
    return noise.reshape(BATCH, STEPS, QH * HD).astype(jnp.bfloat16)


def draw_cache_lengths(key, part):
    long_len = jax.random.randint(jax.random.fold_in(key, 11), (BATCH,), CACHE // 2, CACHE + 1)
    short_len = jax.random.randint(jax.random.fold_in(key, 12), (BATCH,), 1, max(CACHE // 32, 4) + 1)
    pick = jax.random.randint(jax.random.fold_in(key, 13), (BATCH,), 0, 4)
    lengths = jnp.where(pick == 0, short_len, long_len)
    full = jax.random.randint(jax.random.fold_in(key, 14), (), 0, BATCH)
    return lengths.at[full].set(CACHE).astype(jnp.int32)


def touch_ends(result, stream_key, least, top_value):
    longest = result.shape.index(max(result.shape))
    spots = []
    for shift in (0, 1):
        where = [jax.random.randint(jax.random.fold_in(stream_key, axis), (), 0, length) for axis, length in enumerate(result.shape)]
        where[longest] = (where[longest] + shift) % result.shape[longest]
        spots.append(tuple(where))
    return result.at[spots[0]].set(least).at[spots[1]].set(top_value)


def spiked(entries, key, source, target, blocks, factor):
    def block_of(dim):
        return (jnp.arange(entries.shape[dim]) // (entries.shape[dim] // blocks)).reshape((-1,) + (1,) * (entries.ndim - 1 - dim))

    first = jax.random.permutation(key, blocks)[block_of(target)]
    far = (block_of(target) + blocks // 2) % blocks
    return jnp.where((block_of(source) == first) | (block_of(source) == far), factor * entries, entries)


def levels(own_key, dims, cuts, smallest, largest):
    gain, own = 1.0, jax.random.fold_in(own_key, 6)
    for axis_at, shards_of in cuts:
        heights = jnp.exp(jax.random.uniform(jax.random.fold_in(own, axis_at), (shards_of,), jnp.float32, smallest / len(cuts), largest / len(cuts)))
        gain = gain * jnp.repeat(heights, dims[axis_at] // shards_of).reshape([-1 if axis == axis_at else 1 for axis in range(len(dims))])
    return gain


def centred(rng, shape, spread, limit, pieces=(), kind=jnp.bfloat16):
    drawn = jax.random.normal(rng, shape, jnp.float32) * spread
    if len(pieces) > 0:
        drawn = levels(rng, shape, pieces, -0.22, 0.18) * drawn
    return jnp.clip(drawn, min=-limit, max=limit).astype(kind)


def bell_draw_with(own_key, extent, deviation, reach, shards, heavy, kind=jnp.bfloat16):
    values = deviation * jax.random.normal(own_key, extent, jnp.float32)
    if shards:
        values = values * levels(own_key, extent, shards, -0.22, 0.18)
    return jnp.clip(spiked(values, jax.random.fold_in(own_key, 3), *heavy), -reach, reach).astype(kind)


def setup_inputs(seed: int = 0) -> dict:
    key_list = jax.random.split(jax.random.key(seed), 11)
    return {
        "tokens": bell_draw_with(key_list[0], (TOKENS, D), 1.0, 16.0, ((0, 64), (1, 4)), (0, 1, 64, 4.0)),
        "cotangent": centred(key_list[1], (TOKENS, KVW), 1.0, 6.0, ((0, 64), (1, 4))),
        "response_mask": touch_ends((jax.random.randint(key_list[2], (TOKENS,), 0, 4) < 3).astype(jnp.int32), jax.random.fold_in(key_list[2], 1), 0, 1),
        "key_weight": centred(key_list[3], (D, KVW), D ** -0.5, 0.0625, ((0, 64), (1, 4))),
        "new_hidden": centred(key_list[4], (BATCH, STEPS, D), 1.0, 6.0, ((0, 64),)),
        "new_values": centred(key_list[5], (BATCH, STEPS, KVW), 1.0, 6.0, ((0, 64), (2, 4))),
        "queries": draw_queries(jax.random.fold_in(key_list[10], 71), 0),
        "cache_keys": draw_cache_keys(jax.random.fold_in(key_list[10], 71), 0),
        "cache_values": centred(key_list[8], (BATCH, CACHE, KVW), 1.0, 6.0, ((0, 64), (2, 4))),
        "cache_lengths": draw_cache_lengths(jax.random.fold_in(key_list[10], 71), 0),
    }


ROPE_BASE = 1000000.0

def rope_rotate(keys, positions):
    half = keys.shape[-1] // 2
    freq = ROPE_BASE ** (-jnp.arange(half, dtype=jnp.float32) * (2.0 / keys.shape[-1]))
    angle = positions.astype(jnp.float32)[..., None] * freq
    cosine = jnp.cos(angle)[..., None, :]
    sine = jnp.sin(angle)[..., None, :]
    first = keys[..., :half]
    second = keys[..., half:]
    return jnp.concatenate([first * cosine - second * sine, second * cosine + first * sine], axis=-1)

def lifted(array):
    return array.astype(jnp.float32)

def attend(queries, cache_keys, cache_values, new_keys, new_values, lengths):
    count, steps = (queries.shape[0], queries.shape[1])
    slots = cache_keys.shape[1]
    groups = cache_keys.shape[2] // HD
    share = queries.shape[2] // cache_keys.shape[2]
    inv = 1.0 / math.sqrt(HD)
    query = lifted(queries).reshape(count, steps, groups, share, HD)
    old_keys = lifted(cache_keys).reshape(count, slots, groups, HD)
    old_values = lifted(cache_values).reshape(count, slots, groups, HD)
    fresh_keys = lifted(new_keys).reshape(count, steps, groups, HD)
    fresh_values = lifted(new_values).reshape(count, steps, groups, HD)
    cache_scores = jnp.einsum('rsjgd,rcjd->rsjgc', query, old_keys, preferred_element_type=jnp.float32) * inv
    fresh_scores = jnp.einsum('rsjgd,rtjd->rsjgt', query, fresh_keys, preferred_element_type=jnp.float32) * inv
    cache_valid = jnp.arange(slots, dtype=jnp.int32)[None, :] < lengths[:, None]
    step_ids = jnp.arange(steps, dtype=jnp.int32)
    fresh_valid = step_ids[None, :] <= step_ids[:, None]
    cache_scores = jnp.where(cache_valid[:, None, None, None, :], cache_scores, -jnp.inf)
    fresh_scores = jnp.where(fresh_valid[None, :, None, None, :], fresh_scores, -jnp.inf)
    top = jnp.maximum(lax.optimization_barrier(jnp.max(cache_scores, axis=-1)), lax.optimization_barrier(jnp.max(fresh_scores, axis=-1)))[..., None]
    cache_exp = jnp.exp(cache_scores - top)
    fresh_exp = jnp.exp(fresh_scores - top)
    total = lax.optimization_barrier(jnp.sum(cache_exp, axis=-1, keepdims=True)) + lax.optimization_barrier(jnp.sum(fresh_exp, axis=-1, keepdims=True))
    cache_weights = (cache_exp / total).astype(jnp.bfloat16)
    fresh_weights = (fresh_exp / total).astype(jnp.bfloat16)
    mixed = jnp.einsum('rsjgc,rcjd->rsjgd', lifted(cache_weights), old_values, preferred_element_type=jnp.float32)
    mixed = mixed + jnp.einsum('rsjgt,rtjd->rsjgd', lifted(fresh_weights), fresh_values, preferred_element_type=jnp.float32)
    return mixed.reshape(count, steps, groups * share * HD).astype(jnp.bfloat16)

def reference(tokens, cotangent, response_mask, key_weight, new_hidden, new_values, queries, cache_keys, cache_values, cache_lengths):
    masked = cotangent * response_mask[:, None].astype(jnp.bfloat16)
    grad = jnp.dot(tokens.T, masked, preferred_element_type=jnp.float32)
    width = KVW // N_TP
    summed = jnp.zeros((TOKENS, D), jnp.float32)
    for block in range(N_TP):
        part_terms = jnp.dot(masked[:, block * width:(block + 1) * width], key_weight[:, block * width:(block + 1) * width].T, preferred_element_type=jnp.float32)
        summed = summed + part_terms.astype(jnp.bfloat16).astype(jnp.float32)
    grad_inputs = summed.astype(jnp.bfloat16)
    scale = 1.0 / math.sqrt(D * TOKENS)
    learner_weight = (key_weight.astype(jnp.float32) - grad * scale).astype(jnp.bfloat16)
    raw = jnp.dot(new_hidden.reshape(BATCH * STEPS, D), learner_weight, preferred_element_type=jnp.float32)
    raw = raw.reshape(BATCH, STEPS, KVH, HD)
    positions = cache_lengths[:, None] + jnp.arange(STEPS, dtype=jnp.int32)[None, :]
    new_keys = rope_rotate(raw, positions).astype(jnp.bfloat16).reshape(BATCH, STEPS, KVW)

    def one_request(items):
        query, old_k, old_v, fresh_k, fresh_v, length = items
        return attend(query[None], old_k[None], old_v[None], fresh_k[None], fresh_v[None], length[None])[0]
    context = lax.map(one_request, (queries, cache_keys, cache_values, new_keys, new_values, cache_lengths))
    return (grad_inputs, learner_weight, new_keys, context)
```

```python
import math

import jax
import jax.numpy as jnp
from jax import lax
from jax.sharding import Mesh, PartitionSpec as P

D = 8192
HD = 128
NZ, NX, NY, NL, NC = 8, 2, 4, 2, 2
FSDP = ("z", "xh", "y")
TP = ("xl", "c")
F32 = jnp.float32
BF16 = jnp.bfloat16

ROPE_BASE = 1000000.0


def rope_rotate(keys, positions):
    half = keys.shape[-1] // 2
    freq = ROPE_BASE ** (-jnp.arange(half, dtype=jnp.float32) * (2.0 / keys.shape[-1]))
    angle = positions.astype(jnp.float32)[..., None] * freq
    cosine = jnp.cos(angle)[..., None, :]
    sine = jnp.sin(angle)[..., None, :]
    first = keys[..., :half]
    second = keys[..., half:]
    return jnp.concatenate(
        [first * cosine - second * sine, second * cosine + first * sine], axis=-1
    )


def shift(x, axis, size, step):
    return lax.ppermute(x, axis, [(i, (i + step) % size) for i in range(size)])


def swap_owner(x):
    pairs = []
    for z in range(NZ):
        for t in range(NL * NC):
            pairs.append((z * 4 + t, (2 * t + z % 2) * 4 + z // 2))
    return lax.ppermute(x, ("z", "xl", "c"), pairs)


def pick(x, index, axis):
    return lax.dynamic_index_in_dim(x, index, axis, keepdims=False)


def put(buffer, x, index, axis):
    return lax.dynamic_update_index_in_dim(buffer, x, index, axis)


def ring_sum(chunk, axis, size, me):
    far, near = size // 2, size - 1 - size // 2

    def walk(half, hops, sign):
        total = chunk((me + sign * hops) % size, half).astype(BF16)
        for hop in range(hops):
            total = shift(total, axis, size, sign)
            if hop < hops - 1:
                own = chunk((me + sign * (hops - 1 - hop)) % size, half)
                total = (total.astype(F32) + own).astype(BF16)
        return total.astype(F32)

    halves = []
    for half, (up, down) in enumerate(((far, near), (near, far))):
        halves.append(chunk(me, half) + walk(half, up, 1) + walk(half, down, -1))
    return halves


def ring_gather(x, axis, size, me, at):
    shape = x.shape[:at] + (size,) + x.shape[at:]
    buffer = put(jnp.zeros(shape, x.dtype), x, me, at)
    up = down = x
    for hop in range(1, size // 2):
        up = shift(up, axis, size, 1)
        down = shift(down, axis, size, -1)
        buffer = put(buffer, up, (me - hop) % size, at)
        buffer = put(buffer, down, (me + hop) % size, at)
    rows = x.shape[-2] // 2
    low = shift(up[..., :rows, :], axis, size, 1)
    high = shift(down[..., rows:, :], axis, size, -1)
    far = jnp.concatenate([low, high], axis=-2)
    return put(buffer, far, (me + size // 2) % size, at)


def attend_cache(queries, cache_keys, cache_values, lengths):
    count, steps = queries.shape[0], queries.shape[1]
    slots = cache_keys.shape[1]
    groups = cache_keys.shape[2] // HD
    share = queries.shape[2] // cache_keys.shape[2]
    inv = 1.0 / math.sqrt(HD)
    query = queries.reshape(count, steps, groups, share, HD)
    old_keys = cache_keys.reshape(count, slots, groups, HD)
    old_values = cache_values.reshape(count, slots, groups, HD)
    scores = jnp.einsum("rsjgd,rcjd->rsjgc", query, old_keys, preferred_element_type=F32) * inv
    valid = jnp.arange(slots, dtype=jnp.int32)[None, :] < lengths[:, None]
    scores = jnp.where(valid[:, None, None, None, :], scores, -jnp.inf)
    top = jnp.max(scores, axis=-1, keepdims=True)
    weight = jnp.exp(scores - top)
    total = jnp.sum(weight, axis=-1, keepdims=True)
    mixed = jnp.einsum(
        "rsjgc,rcjd->rsjgd", weight.astype(BF16), old_values, preferred_element_type=F32
    )
    return top, total, mixed


def attend_fresh(queries, new_keys, new_values, top, total, mixed):
    count, steps = queries.shape[0], queries.shape[1]
    groups = new_keys.shape[2] // HD
    share = queries.shape[2] // new_keys.shape[2]
    inv = 1.0 / math.sqrt(HD)
    query = queries.reshape(count, steps, groups, share, HD)
    fresh_keys = new_keys.reshape(count, steps, groups, HD)
    fresh_values = new_values.reshape(count, steps, groups, HD)
    scores = jnp.einsum("rsjgd,rtjd->rsjgt", query, fresh_keys, preferred_element_type=F32) * inv
    step_ids = jnp.arange(steps, dtype=jnp.int32)
    valid = step_ids[None, :] <= step_ids[:, None]
    scores = jnp.where(valid[None, :, None, None, :], scores, -jnp.inf)
    high = jnp.maximum(top, jnp.max(scores, axis=-1, keepdims=True))
    old = jnp.exp(top - high)
    weight = jnp.exp(scores - high)
    whole = total * old + jnp.sum(weight, axis=-1, keepdims=True)
    fresh = jnp.einsum(
        "rsjgt,rtjd->rsjgd", weight.astype(BF16), fresh_values, preferred_element_type=F32
    )
    context = (mixed * old + fresh) / whole
    return context.reshape(count, steps, groups * share * HD).astype(BF16)


def per_device(
    tokens,
    cotangent,
    response_mask,
    key_weight,
    new_hidden,
    new_values,
    queries,
    cache_keys,
    cache_values,
    cache_lengths,
):
    z, xh, y = lax.axis_index("z"), lax.axis_index("xh"), lax.axis_index("y")
    xl, c = lax.axis_index("xl"), lax.axis_index("c")
    tp = xl * NC + c
    odd = z % 2
    wide = tokens.shape[1]
    cols = cotangent.shape[1]
    rows = key_weight.shape[0]
    requests, steps = new_hidden.shape[0], new_hidden.shape[1]
    lines = requests * steps

    masked = cotangent * response_mask[:, None].astype(BF16)
    masked_all = lax.all_gather(masked, TP, axis=1, tiled=True)

    hidden = new_hidden.reshape(lines, new_hidden.shape[2])
    hidden = lax.dynamic_slice_in_dim(hidden, tp * wide, wide, 1)
    hidden = hidden.reshape(lines, 2, NX, NY, rows)
    part = put(jnp.zeros((NY, lines, 2, NX, rows), BF16), pick(hidden, y, 3), y, 0)
    for step in range(1, NY):
        got = shift(pick(hidden, (y + step) % NY, 3), "y", NY, step)
        part = put(part, got, (y - step) % NY, 0)
    got = shift(pick(part, 1 - xh, 3), "xh", NX, 1)
    both = put(jnp.zeros((NX, NY, lines, 2, rows), BF16), pick(part, xh, 3), xh, 0)
    part = put(both, got, 1 - xh, 0)
    every = put(jnp.zeros((NZ, NX, NY, lines, rows), BF16), pick(part, odd, 3), z, 0)
    for step in range(1, NZ):
        got = shift(pick(part, (z + step) % 2, 3), "z", NZ, step)
        every = put(every, got, (z - step) % NZ, 0)

    own_weight = swap_owner(key_weight)
    old = ring_gather(own_weight, "z", NZ, z, 0)
    old = old.reshape(NL * NC, 2, rows, cols).transpose(1, 2, 0, 3).reshape(2, rows, NL * NC * cols)
    other = shift(old, "xh", NX, 1)
    both = put(jnp.zeros((2, NX) + old.shape[1:], BF16), old, xh, 1)
    old = put(both, other, 1 - xh, 1)
    old = ring_gather(old, "y", NY, y, 2)
    old = old.reshape(wide, NL * NC * cols)

    def term(k, half):
        left = lax.dynamic_slice_in_dim(tokens, (k % 2) * (wide // 2) + half * (wide // 4), wide // 4, 1)
        right = lax.dynamic_slice_in_dim(masked_all, (k // 2) * cols, cols, 1)
        return lax.dot_general(left, right, (((0,), (0,)), ((), ())), preferred_element_type=F32)

    halves = ring_sum(term, "z", NZ, z)
    blocks = [h.reshape(NY, rows, cols) for h in halves]
    halves = ring_sum(lambda k, half: pick(blocks[half], k, 0), "y", NY, y)
    pair = jnp.stack(halves)
    grad = pick(pair, xh, 0) + shift(pick(pair, 1 - xh, 0).astype(BF16), "xh", NX, 1).astype(F32)

    scale = 1.0 / math.sqrt(D * tokens.shape[0] * NZ * NX * NY)
    own_weight = (own_weight.astype(F32) - grad * scale).astype(BF16)
    learner_weight = swap_owner(own_weight)

    def raw_term(k, half):
        left = pick(every[:, half], k, 1).reshape(NZ * lines, rows)
        return jnp.dot(left, own_weight, preferred_element_type=F32)

    pair = jnp.stack(ring_sum(raw_term, "y", NY, y))
    raw = pick(pair, xh, 0) + shift(pick(pair, 1 - xh, 0).astype(BF16), "xh", NX, 1).astype(F32)
    raw = raw.reshape(NL, NC, 2, lines, cols)
    raw = pick(raw, c, 1) + shift(pick(raw, 1 - c, 1), "c", NC, 1)
    raw = pick(raw, xl, 0) + shift(pick(raw, 1 - xl, 0), "xl", NL, 1)
    near = lax.ppermute(pick(raw, 1 - odd, 0), "z", [(i, i ^ 1) for i in range(NZ)])
    raw = swap_owner(pick(raw, odd, 0) + near)

    positions = cache_lengths[:, None] + jnp.arange(steps, dtype=jnp.int32)[None, :]
    rotated = rope_rotate(raw.reshape(requests, steps, cols // HD, HD), positions)
    new_keys = rotated.astype(BF16).reshape(requests, steps, cols)

    top, total, mixed = attend_cache(queries, cache_keys, cache_values, cache_lengths)
    context = attend_fresh(queries, new_keys, new_values, top, total, mixed)

    grad_inputs = lax.dot_general(
        masked_all, old, (((1,), (1,)), ((), ())), preferred_element_type=F32
    ).astype(BF16)
    return (grad_inputs, learner_weight, new_keys, context)


def solution(mesh):
    split = Mesh(mesh.devices.reshape(NZ, NX, NY, NL, NC), ("z", "xh", "y", "xl", "c"))
    placed = (
        P(FSDP, TP),
        P(FSDP, TP),
        P(FSDP),
        P(FSDP, TP),
        P(FSDP, None, None),
        P(FSDP, None, TP),
        P(FSDP, None, TP),
        P(FSDP, None, TP),
        P(FSDP, None, TP),
        P(FSDP),
    )
    return jax.shard_map(
        per_device,
        mesh=split,
        in_specs=placed,
        out_specs=(P(FSDP, TP), P(FSDP, TP), P(FSDP, None, TP), P(FSDP, None, TP)),
        check_vma=False,
    )
```

```python
import math

import jax
import jax.numpy as jnp
from jax import lax
from jax.experimental import pallas as pl
from jax.experimental.pallas import tpu as pltpu
from jax.sharding import Mesh, PartitionSpec as P


D = 8192
HD = 128
NZ, NX, NY, NL, NC = 8, 2, 4, 2, 2
FSDP = ("z", "xh", "y")
TP = ("xl", "c")
F32 = jnp.float32
BF16 = jnp.bfloat16

ROPE_BASE = 1000000.0


def shift(x, axis, size, step):
    return lax.ppermute(x, axis, [(i, (i + step) % size) for i in range(size)])


def swap_owner(x, flip=0):
    pairs = []
    for z in range(NZ):
        for t in range(NL * NC):
            pairs.append((z * 4 + t, (2 * t + (z % 2 ^ flip)) * 4 + z // 2))
    return lax.ppermute(x, ("z", "xl", "c"), pairs)


def pick(x, index, axis):
    return lax.dynamic_index_in_dim(x, index, axis, keepdims=False)


def ring_sum(term, axis, size, me):
    last = size // 2
    whole = term((me + last) & (size - 1)).astype(BF16)
    half = whole.shape[0] // 2
    up, down = whole[:half], whole[half:]
    for hop in range(last, 0, -1):
        if hop < last:
            plus, minus = term((me + hop) & (size - 1)), term((me - hop) & (size - 1))
            up, down = up.astype(F32), down.astype(F32)
            if hop == last - 1:
                up = jnp.pad(up, [(0, half)] + [(0, 0)] * (up.ndim - 1))
                down = jnp.pad(down, [(half, 0)] + [(0, 0)] * (down.ndim - 1))
            up, down = (plus + up).astype(BF16), (minus + down).astype(BF16)
        up = shift(up, axis, size, 1)
        down = shift(down, axis, size, -1)
    return term(me) + up.astype(F32) + down.astype(F32)


def stacked(flat, share):
    wide = flat.astype(F32)
    return jnp.concatenate([wide[:, h * HD : (h + 1) * HD] for h in range(share)], axis=0)


def cache_kernel(lengths, q_ref, k_ref, v_ref, mixed_ref, top_ref, total_ref, *, share):
    valid = lengths[pl.program_id(0)]
    query = stacked(q_ref[0], share).astype(BF16)
    scores = lax.dot_general(
        query, k_ref[0], (((1,), (1,)), ((), ())), preferred_element_type=F32
    ) * (1.0 / math.sqrt(HD))
    slot = lax.broadcasted_iota(jnp.int32, scores.shape, 1)
    scores = jnp.where(slot < valid, scores, -jnp.inf)
    top = jnp.max(scores, axis=1, keepdims=True)
    weight = jnp.exp(scores - top)
    total = jnp.sum(weight, axis=1, keepdims=True)
    mixed_ref[0, 0] = jnp.dot(weight.astype(BF16), v_ref[0], preferred_element_type=F32)
    top_ref[0, 0] = jnp.broadcast_to(top, top_ref.shape[2:])
    total_ref[0, 0] = jnp.broadcast_to(total, total_ref.shape[2:])


def attend_cache(queries, cache_keys, cache_values, lengths):
    count, steps, width = queries.shape
    slots = cache_keys.shape[1]
    groups = cache_keys.shape[2] // HD
    share = width // cache_keys.shape[2]
    state = jax.ShapeDtypeStruct((count, groups, share * steps, HD), F32)
    state_spec = pl.BlockSpec((1, 1, share * steps, HD), lambda r, j, n: (r, j, 0, 0))
    cache_spec = pl.BlockSpec((1, slots, HD), lambda r, j, n: (r, 0, j))
    return pl.pallas_call(
        lambda *refs: cache_kernel(*refs, share=share),
        out_shape=(state, state, state),
        grid_spec=pltpu.PrefetchScalarGridSpec(
            num_scalar_prefetch=1,
            grid=(count, groups),
            in_specs=[
                pl.BlockSpec((1, steps, share * HD), lambda r, j, n: (r, 0, j)),
                cache_spec,
                cache_spec,
            ],
            out_specs=[state_spec, state_spec, state_spec],
        ),
        cost_estimate=pl.CostEstimate(
            flops=4 * count * groups * share * steps * slots * HD,
            bytes_accessed=4 * count * slots * groups * HD,
            transcendentals=count * groups * share * steps * slots,
        ),
        name="cache_attention",
    )(lengths, queries, cache_keys, cache_values)


def fresh_kernel(
    raw_ref, cos_ref, sin_ref, q_ref, v_ref, mixed_ref, top_ref, total_ref, keys_ref, out_ref, *, share
):
    raw = raw_ref[...]
    keys = raw * cos_ref[...] + pltpu.roll(raw, HD // 2, 1) * sin_ref[...]
    keys = keys.astype(BF16)
    keys_ref[0] = keys
    steps = keys.shape[0]
    query = stacked(q_ref[0], share).astype(BF16)
    scores = lax.dot_general(
        query, keys, (((1,), (1,)), ((), ())), preferred_element_type=F32
    ) * (1.0 / math.sqrt(HD))
    step = lax.broadcasted_iota(jnp.int32, scores.shape, 0) % steps
    scores = jnp.where(lax.broadcasted_iota(jnp.int32, scores.shape, 1) <= step, scores, -jnp.inf)
    top = top_ref[0, 0]
    high = jnp.maximum(top, jnp.max(scores, axis=1, keepdims=True))
    old = jnp.exp(top - high)
    weight = jnp.exp(scores - high[:, :1])
    whole = total_ref[0, 0] * old + jnp.sum(weight, axis=1, keepdims=True)
    fresh = jnp.dot(weight.astype(BF16), v_ref[0], preferred_element_type=F32)
    context = ((mixed_ref[0, 0] * old + fresh) / whole).astype(BF16).astype(F32)
    flat = [context[h * steps : (h + 1) * steps] for h in range(share)]
    out_ref[0] = jnp.concatenate(flat, axis=1).astype(BF16)


def attend_fresh(raw, cosine, sine, queries, new_values, mixed, top, total):
    count, steps, width = queries.shape
    groups = new_values.shape[2] // HD
    share = width // new_values.shape[2]
    state_spec = pl.BlockSpec((1, 1, share * steps, HD), lambda r, j: (r, j, 0, 0))
    query_spec = pl.BlockSpec((1, steps, share * HD), lambda r, j: (r, 0, j))
    value_spec = pl.BlockSpec((1, steps, HD), lambda r, j: (r, 0, j))
    angle_spec = pl.BlockSpec((steps, HD), lambda r, j: (r, 0))
    return pl.pallas_call(
        lambda *refs: fresh_kernel(*refs, share=share),
        out_shape=(
            jax.ShapeDtypeStruct(new_values.shape, BF16),
            jax.ShapeDtypeStruct(queries.shape, BF16),
        ),
        grid=(count, groups),
        in_specs=[
            pl.BlockSpec((steps, HD), lambda r, j: (r, j)),
            angle_spec,
            angle_spec,
            query_spec,
            value_spec,
            state_spec,
            state_spec,
            state_spec,
        ],
        out_specs=[value_spec, query_spec],
        name="fresh_attention",
    )(raw, cosine, sine, queries, new_values, mixed, top, total)


def input_kernel(m_ref, w_ref, out_ref):
    blocks, cols = w_ref.shape[2], w_ref.shape[5]
    total = jnp.zeros(out_ref.shape, F32)
    for block in range(blocks):
        total += lax.dot_general(
            m_ref[:, block * cols : (block + 1) * cols],
            w_ref[0, 0, block, 0],
            (((1,), (1,)), ((), ())),
            preferred_element_type=F32,
        )
    out_ref[...] = total.astype(BF16)


def input_grad(masked, weight):
    ny, nx, blocks, two, rows, cols = weight.shape
    count = masked.shape[0]
    return pl.pallas_call(
        input_kernel,
        out_shape=jax.ShapeDtypeStruct((count, two * nx * ny * rows), BF16),
        grid=(ny, nx, two),
        in_specs=[
            pl.BlockSpec((count, blocks * cols), lambda i, k, j: (0, 0)),
            pl.BlockSpec((1, 1, blocks, 1, rows, cols), lambda i, k, j: (i, k, 0, j, 0, 0)),
        ],
        out_specs=pl.BlockSpec((count, rows), lambda i, k, j: (0, (j * nx + k) * ny + i)),
        cost_estimate=pl.CostEstimate(
            flops=2 * count * weight.size, bytes_accessed=2 * weight.size, transcendentals=0
        ),
        name="input_grad",
    )(masked, weight)


def angles(lengths, steps):
    half = HD // 2
    freq = ROPE_BASE ** (-jnp.arange(half, dtype=F32) * (2.0 / HD))
    positions = lengths[:, None] + jnp.arange(steps, dtype=jnp.int32)[None, :]
    angle = positions.reshape(-1).astype(F32)[:, None] * freq
    cosine, sine = jnp.cos(angle), jnp.sin(angle)
    return jnp.concatenate([cosine, cosine], axis=1), jnp.concatenate([-sine, sine], axis=1)


def update_and_decode(
    tokens,
    cotangent,
    response_mask,
    key_weight,
    new_hidden,
    new_values,
    queries,
    cache_keys,
    cache_values,
    cache_lengths,
):
    z, xh, y = lax.axis_index("z"), lax.axis_index("xh"), lax.axis_index("y")
    xl, c = lax.axis_index("xl"), lax.axis_index("c")
    tp = xl * NC + c
    odd = z & 1
    wide = tokens.shape[1]
    cols = cotangent.shape[1]
    rows = key_weight.shape[0]
    requests, steps = new_hidden.shape[0], new_hidden.shape[1]
    lines = requests * steps

    masked = cotangent * response_mask[:, None].astype(BF16)
    masked_all = lax.all_gather(masked, TP, axis=1, tiled=True)

    hidden = new_hidden.reshape(lines, new_hidden.shape[2])
    hidden = lax.dynamic_slice_in_dim(hidden, tp * wide, wide, 1)
    hidden = hidden.reshape(lines, 2, NX * NY, rows).transpose(2, 1, 0, 3)
    hidden = lax.all_to_all(hidden, ("xh", "y"), 0, 0, tiled=True)
    hidden = hidden.transpose(1, 0, 2, 3).reshape(1, 2, NX * NY * lines, rows)
    hidden = jnp.broadcast_to(hidden, (NZ // 2,) + hidden.shape[1:]).reshape(NZ, NX * NY * lines, rows)
    hidden = lax.all_to_all(hidden, "z", 0, 0, tiled=True)
    hidden = hidden.reshape(NZ, NX, NY, lines, rows)

    own_weight = swap_owner(key_weight)
    old = lax.all_gather(own_weight, "z")
    old = lax.all_gather(old, "xh")
    old = lax.all_gather(old, "y")
    old = old.reshape(NY, NX, NL * NC, 2, rows, cols)

    def term(k):
        left = lax.dynamic_slice_in_dim(tokens, (k & 1) * (wide // 2), wide // 2, 1)
        right = lax.dynamic_slice_in_dim(masked_all, (k >> 1) * cols, cols, 1)
        return lax.dot_general(left, right, (((0,), (0,)), ((), ())), preferred_element_type=F32)

    part = ring_sum(term, "z", NZ, z).reshape(NX, NY, rows, cols)
    part = ring_sum(lambda k: pick(part, k, 1), "y", NY, y)
    other = shift(pick(part, 1 - xh, 0).astype(BF16), "xh", NX, 1)
    grad = pick(part, xh, 0) + other.astype(F32)

    scale = 1.0 / math.sqrt(D * tokens.shape[0] * NZ * NX * NY)
    own_weight = (own_weight.astype(F32) - grad * scale).astype(BF16)

    def raw_term(k):
        left = pick(hidden, k, 2).reshape(NZ * NX * lines, rows)
        return jnp.dot(left, own_weight, preferred_element_type=F32)

    raw = ring_sum(raw_term, "y", NY, y).reshape(NL, NC, 2, NX, lines, cols)
    other = shift(pick(raw, 1 - xh, 3).astype(BF16), "xh", NX, 1)
    raw = pick(raw, xh, 3) + other.astype(F32)
    other = shift(pick(raw, 1 - c, 1), "c", NC, 1)
    raw = pick(raw, c, 1) + other
    other = shift(pick(raw, 1 - xl, 0), "xl", NL, 1)
    raw = pick(raw, xl, 0) + other
    same = swap_owner(pick(raw, odd, 0))
    other = swap_owner(pick(raw, 1 - odd, 0), 1)
    raw = same + other

    learner_weight = swap_owner(own_weight)

    state = attend_cache(queries, cache_keys, cache_values, cache_lengths)
    cosine, sine = angles(cache_lengths, steps)
    new_keys, context = attend_fresh(raw, cosine, sine, queries, new_values, *state)

    grad_inputs = input_grad(masked_all, old)
    return (grad_inputs, learner_weight, new_keys, context)


def solution(mesh):
    split = Mesh(mesh.devices.reshape(NZ, NX, NY, NL, NC), ("z", "xh", "y", "xl", "c"))
    placed = (
        P(FSDP, TP),
        P(FSDP, TP),
        P(FSDP),
        P(FSDP, TP),
        P(FSDP, None, None),
        P(FSDP, None, TP),
        P(FSDP, None, TP),
        P(FSDP, None, TP),
        P(FSDP, None, TP),
        P(FSDP),
    )
    return jax.shard_map(
        update_and_decode,
        mesh=split,
        in_specs=placed,
        out_specs=(P(FSDP, TP), P(FSDP, TP), P(FSDP, None, TP), P(FSDP, None, TP)),
        check_vma=False,
    )
```

```python
import math

import jax
import jax.numpy as jnp
from jax import lax
from jax.experimental import pallas as pl
from jax.experimental.pallas import tpu as pltpu
from jax.sharding import Mesh, PartitionSpec as P


D = 8192
HD = 128
NZ, NX, NY, NL, NC = 8, 2, 4, 2, 2
FSDP = ("z", "xh", "y")
TP = ("xl", "c")
F32 = jnp.float32
BF16 = jnp.bfloat16

ROPE_BASE = 1000000.0


def shift(x, axis, size, step):
    return lax.ppermute(x, axis, [(i, (i + step) % size) for i in range(size)])


def swap_owner(x, flip=0):
    pairs = []
    for z in range(NZ):
        for t in range(NL * NC):
            pairs.append((z * 4 + t, (2 * t + (z % 2 ^ flip)) * 4 + z // 2))
    return lax.ppermute(x, ("z", "xl", "c"), pairs)


def pick(x, index, axis):
    return lax.dynamic_index_in_dim(x, index, axis, keepdims=False)


def ring_sum(term, axis, size, me):
    last = size // 2
    whole = term((me + last) & (size - 1)).astype(BF16)
    half = whole.shape[0] // 2
    up, down = whole[:half], whole[half:]
    for hop in range(last, 0, -1):
        if hop < last:
            plus, minus = term((me + hop) & (size - 1)), term((me - hop) & (size - 1))
            up, down = up.astype(F32), down.astype(F32)
            if hop == last - 1:
                up = jnp.pad(up, [(0, half)] + [(0, 0)] * (up.ndim - 1))
                down = jnp.pad(down, [(half, 0)] + [(0, 0)] * (down.ndim - 1))
            up, down = (plus + up).astype(BF16), (minus + down).astype(BF16)
        up = shift(up, axis, size, 1)
        down = shift(down, axis, size, -1)
    return term(me) + up.astype(F32) + down.astype(F32)


def stacked(flat, share):
    wide = flat.astype(F32)
    return jnp.concatenate([wide[:, h * HD : (h + 1) * HD] for h in range(share)], axis=0)


def cache_kernel(lengths, q_ref, k_ref, v_ref, mixed_ref, top_ref, total_ref, *, share):
    valid = lengths[pl.program_id(0)]
    query = stacked(q_ref[0], share).astype(BF16)
    scores = lax.dot_general(
        query, k_ref[0], (((1,), (1,)), ((), ())), preferred_element_type=F32
    ) * (1.0 / math.sqrt(HD))
    slot = lax.broadcasted_iota(jnp.int32, scores.shape, 1)
    scores = jnp.where(slot < valid, scores, -jnp.inf)
    top = jnp.max(scores, axis=1, keepdims=True)
    weight = jnp.exp(scores - top)
    total = jnp.sum(weight, axis=1, keepdims=True)
    mixed_ref[0, 0] = jnp.dot(weight.astype(BF16), v_ref[0], preferred_element_type=F32)
    top_ref[0, 0] = jnp.broadcast_to(top, top_ref.shape[2:])
    total_ref[0, 0] = jnp.broadcast_to(total, total_ref.shape[2:])


def attend_cache(queries, cache_keys, cache_values, lengths):
    count, steps, width = queries.shape
    slots = cache_keys.shape[1]
    groups = cache_keys.shape[2] // HD
    share = width // cache_keys.shape[2]
    state = jax.ShapeDtypeStruct((count, groups, share * steps, HD), F32)
    state_spec = pl.BlockSpec((1, 1, share * steps, HD), lambda r, j, n: (r, j, 0, 0))
    cache_spec = pl.BlockSpec((1, slots, HD), lambda r, j, n: (r, 0, j))
    return pl.pallas_call(
        lambda *refs: cache_kernel(*refs, share=share),
        out_shape=(state, state, state),
        grid_spec=pltpu.PrefetchScalarGridSpec(
            num_scalar_prefetch=1,
            grid=(count, groups),
            in_specs=[
                pl.BlockSpec((1, steps, share * HD), lambda r, j, n: (r, 0, j)),
                cache_spec,
                cache_spec,
            ],
            out_specs=[state_spec, state_spec, state_spec],
        ),
        cost_estimate=pl.CostEstimate(
            flops=4 * count * groups * share * steps * slots * HD,
            bytes_accessed=4 * count * slots * groups * HD,
            transcendentals=count * groups * share * steps * slots,
        ),
        name="cache_attention",
    )(lengths, queries, cache_keys, cache_values)


def fresh_kernel(
    same_ref, other_ref, cos_ref, sin_ref, q_ref, v_ref, mixed_ref, top_ref, total_ref, keys_ref, out_ref
):
    count, steps, width = q_ref.shape
    groups = v_ref.shape[2] // HD
    share = width // v_ref.shape[2]
    for r in range(count):
        lines = slice(r * steps, (r + 1) * steps)
        for j in range(groups):
            lanes = slice(j * HD, (j + 1) * HD)
            heads = slice(j * share * HD, (j + 1) * share * HD)
            raw = same_ref[lines, lanes] + other_ref[lines, lanes]
            keys = raw * cos_ref[lines, :] + pltpu.roll(raw, HD // 2, 1) * sin_ref[lines, :]
            keys = keys.astype(BF16)
            keys_ref[r, :, lanes] = keys
            query = stacked(q_ref[r, :, heads], share).astype(BF16)
            scores = lax.dot_general(
                query, keys, (((1,), (1,)), ((), ())), preferred_element_type=F32
            ) * (1.0 / math.sqrt(HD))
            step = lax.broadcasted_iota(jnp.int32, scores.shape, 0) % steps
            seen = lax.broadcasted_iota(jnp.int32, scores.shape, 1) <= step
            scores = jnp.where(seen, scores, -jnp.inf)
            top = top_ref[r, j]
            high = jnp.maximum(top, jnp.max(scores, axis=1, keepdims=True))
            old = jnp.exp(top - high)
            weight = jnp.exp(scores - high[:, :1])
            whole = total_ref[r, j] * old + jnp.sum(weight, axis=1, keepdims=True)
            fresh = jnp.dot(weight.astype(BF16), v_ref[r, :, lanes], preferred_element_type=F32)
            context = (mixed_ref[r, j] * old + fresh) / whole
            flat = [context[h * steps : (h + 1) * steps] for h in range(share)]
            out_ref[r, :, heads] = jnp.concatenate(flat, axis=1).astype(BF16)


def attend_fresh(same, other, cosine, sine, queries, new_values, mixed, top, total):
    return pl.pallas_call(
        fresh_kernel,
        out_shape=(
            jax.ShapeDtypeStruct(new_values.shape, BF16),
            jax.ShapeDtypeStruct(queries.shape, BF16),
        ),
        name="fresh_attention",
    )(same, other, cosine, sine, queries, new_values, mixed, top, total)


def input_kernel(place, m_ref, w_ref, *refs):
    out_ref = refs[-1]
    blocks, cols = w_ref.shape[1], w_ref.shape[4]
    total = jnp.zeros(out_ref.shape, F32)
    for block in range(blocks):
        total += lax.dot_general(
            m_ref[:, block * cols : (block + 1) * cols],
            w_ref[0, block, 0],
            (((1,), (1,)), ((), ())),
            preferred_element_type=F32,
        )
    out_ref[...] = total.astype(BF16)


def input_grad(masked, weight, place, out, wide):
    pieces, blocks, two, rows, cols = weight.shape
    count = masked.shape[0]
    more = [] if out is None else [out]
    return pl.pallas_call(
        input_kernel,
        out_shape=jax.ShapeDtypeStruct((count, wide), BF16),
        grid_spec=pltpu.PrefetchScalarGridSpec(
            num_scalar_prefetch=1,
            grid=(pieces, two),
            in_specs=[
                pl.BlockSpec((count, blocks * cols), lambda q, j, n: (0, 0)),
                pl.BlockSpec((1, blocks, 1, rows, cols), lambda q, j, n: (q, 0, j, 0, 0)),
            ]
            + [pl.BlockSpec(memory_space=pl.ANY) for _ in more],
            out_specs=pl.BlockSpec(
                (count, rows), lambda q, j, n: (0, j * NX * NY + (q ^ n[0]) * NY + n[1])
            ),
        ),
        input_output_aliases={3: 0} if more else {},
        cost_estimate=pl.CostEstimate(
            flops=2 * count * weight.size, bytes_accessed=2 * weight.size, transcendentals=0
        ),
        name="input_grad",
    )(jnp.stack(place).astype(jnp.int32), masked, weight, *more)


def angles(lengths, steps):
    half = HD // 2
    freq = ROPE_BASE ** (-jnp.arange(half, dtype=F32) * (2.0 / HD))
    positions = lengths[:, None] + jnp.arange(steps, dtype=jnp.int32)[None, :]
    angle = positions.reshape(-1).astype(F32)[:, None] * freq
    cosine, sine = jnp.cos(angle), jnp.sin(angle)
    return jnp.concatenate([cosine, cosine], axis=1), jnp.concatenate([-sine, sine], axis=1)


def update_and_decode(
    tokens,
    cotangent,
    response_mask,
    key_weight,
    new_hidden,
    new_values,
    queries,
    cache_keys,
    cache_values,
    cache_lengths,
):
    z, xh, y = lax.axis_index("z"), lax.axis_index("xh"), lax.axis_index("y")
    xl, c = lax.axis_index("xl"), lax.axis_index("c")
    tp = xl * NC + c
    odd = z & 1
    wide = tokens.shape[1]
    cols = cotangent.shape[1]
    rows = key_weight.shape[0]
    requests, steps = new_hidden.shape[0], new_hidden.shape[1]
    lines = requests * steps

    masked = cotangent * response_mask[:, None].astype(BF16)
    masked_all = lax.all_gather(masked, TP, axis=1, tiled=True)

    hidden = new_hidden.reshape(lines, new_hidden.shape[2])
    hidden = lax.dynamic_slice_in_dim(hidden, tp * wide, wide, 1)
    hidden = hidden.reshape(lines, 2, NX * NY, rows).transpose(2, 1, 0, 3)
    hidden = lax.all_to_all(hidden, ("xh", "y"), 0, 0, tiled=True)
    hidden = hidden.transpose(1, 0, 2, 3).reshape(1, 2, NX * NY * lines, rows)
    hidden = jnp.broadcast_to(hidden, (NZ // 2,) + hidden.shape[1:]).reshape(NZ, NX * NY * lines, rows)
    hidden = lax.all_to_all(hidden, "z", 0, 0, tiled=True)
    hidden = hidden.reshape(NZ, NX * NY, lines, rows).transpose(1, 0, 2, 3).reshape(-1, rows)

    own_weight = swap_owner(key_weight)
    old = jnp.broadcast_to(own_weight, (NZ, rows, cols))
    old = lax.all_to_all(old, "z", 0, 0, tiled=True)
    old = old.reshape(NL * NC, 2, rows, cols)
    other = shift(old, "xh", NX, 1)
    old = jnp.stack([old, other])
    up = shift(old, "y", NY, 1)
    down = shift(old, "y", NY, -1)
    far_up = shift(up[:1], "y", NY, 1)
    far_down = shift(down[1:], "y", NY, -1)

    def term(k):
        left = lax.dynamic_slice_in_dim(tokens, (k & 1) * (wide // 2), wide // 2, 1)
        right = lax.dynamic_slice_in_dim(masked_all, (k >> 1) * cols, cols, 1)
        return lax.dot_general(left, right, (((0,), (0,)), ((), ())), preferred_element_type=F32)

    part = ring_sum(term, "z", NZ, z).reshape(NX, NY, rows, cols)
    part = part.astype(BF16).reshape(NX * NY, rows, cols)
    part = lax.all_to_all(part, ("xh", "y"), 0, 0, tiled=True)
    grad = jnp.sum(part.astype(F32), axis=0)

    scale = 1.0 / math.sqrt(D * tokens.shape[0] * NZ * NX * NY)
    own_weight = (own_weight.astype(F32) - grad * scale).astype(BF16)

    raw = jnp.dot(hidden, own_weight, preferred_element_type=F32).astype(BF16)
    raw = raw.reshape(NX * NY, NZ * lines, cols)
    raw = lax.all_to_all(raw, ("xh", "y"), 0, 0, tiled=True)
    raw = jnp.sum(raw.astype(F32), axis=0).reshape(NL, NC, 2, lines, cols)
    other = shift(pick(raw, 1 - c, 1), "c", NC, 1)
    raw = pick(raw, c, 1) + other
    other = shift(pick(raw, 1 - xl, 0), "xl", NL, 1)
    raw = pick(raw, xl, 0) + other
    same = swap_owner(pick(raw, odd, 0))
    other = swap_owner(pick(raw, 1 - odd, 0), 1)

    learner_weight = swap_owner(own_weight)

    state = attend_cache(queries, cache_keys, cache_values, cache_lengths)
    cosine, sine = angles(cache_lengths, steps)
    new_keys, context = attend_fresh(same, other, cosine, sine, queries, new_values, *state)

    grad_inputs = None
    for weight, across, owner in (
        (old, xh, y),
        (up, xh, (y - 1) & (NY - 1)),
        (down, xh, (y + 1) & (NY - 1)),
        (far_up, xh, y ^ 2),
        (far_down, 1 - xh, y ^ 2),
    ):
        grad_inputs = input_grad(masked_all, weight, (across, owner), grad_inputs, wide)
    return (grad_inputs, learner_weight, new_keys, context)


def solution(mesh):
    split = Mesh(mesh.devices.reshape(NZ, NX, NY, NL, NC), ("z", "xh", "y", "xl", "c"))
    placed = (
        P(FSDP, TP),
        P(FSDP, TP),
        P(FSDP),
        P(FSDP, TP),
        P(FSDP, None, None),
        P(FSDP, None, TP),
        P(FSDP, None, TP),
        P(FSDP, None, TP),
        P(FSDP, None, TP),
        P(FSDP),
    )
    return jax.shard_map(
        update_and_decode,
        mesh=split,
        in_specs=placed,
        out_specs=(P(FSDP, TP), P(FSDP, TP), P(FSDP, None, TP), P(FSDP, None, TP)),
        check_vma=False,
    )
```

```python
import math

import jax
import jax.numpy as jnp
from jax import lax
from jax.experimental import pallas as pl
from jax.experimental.pallas import tpu as pltpu
from jax.sharding import Mesh, PartitionSpec as P


D = 8192
HD = 128
NZ, NX, NY, NL, NC = 8, 2, 4, 2, 2
FSDP = ("z", "xh", "y")
TP = ("xl", "c")
F32 = jnp.float32
BF16 = jnp.bfloat16

ROPE_BASE = 1000000.0


def shift(x, axis, size, step):
    return lax.ppermute(x, axis, [(i, (i + step) % size) for i in range(size)])


def swap_owner(x, flip=0):
    pairs = []
    for z in range(NZ):
        for t in range(NL * NC):
            pairs.append((z * 4 + t, (2 * t + (z % 2 ^ flip)) * 4 + z // 2))
    return lax.ppermute(x, ("z", "xl", "c"), pairs)


def pick(x, index, axis):
    return lax.dynamic_index_in_dim(x, index, axis, keepdims=False)


def ring_sum(term, axis, size, me):
    last = size // 2
    whole = term((me + last) & (size - 1)).astype(BF16)
    half = whole.shape[0] // 2
    up, down = whole[:half], whole[half:]

    def low(x):
        return jnp.pad(x, [(0, half), (0, 0)])

    def high(x):
        return jnp.pad(x, [(half, 0), (0, 0)])

    for hop in range(last, 0, -1):
        if hop < last:
            plus, minus = term((me + hop) & (size - 1)), term((me - hop) & (size - 1))
            up, down = up.astype(F32), down.astype(F32)
            if hop == last - 1:
                up, down = low(up), high(down)
            else:
                up, down = low(up[:half]) + high(up[half:]), low(down[:half]) + high(down[half:])
            up, down = (plus + up).astype(BF16), (minus + down).astype(BF16)
        up = shift(up, axis, size, 1)
        down = shift(down, axis, size, -1)
    return term(me) + up.astype(F32) + down.astype(F32)


def stacked(flat, share):
    wide = flat.astype(F32)
    return jnp.concatenate([wide[:, h * HD : (h + 1) * HD] for h in range(share)], axis=0)


def cache_kernel(lengths, q_ref, k_ref, v_ref, mixed_ref, top_ref, total_ref, *, groups, share):
    valid = lengths[pl.program_id(0)]
    for j in range(groups):
        lanes = slice(j * HD, (j + 1) * HD)
        query = stacked(q_ref[0, :, j * share * HD : (j + 1) * share * HD], share).astype(BF16)
        scores = lax.dot_general(
            query, k_ref[0, :, lanes], (((1,), (1,)), ((), ())), preferred_element_type=F32
        ) * (1.0 / math.sqrt(HD))
        slot = lax.broadcasted_iota(jnp.int32, scores.shape, 1)
        scores = jnp.where(slot < valid, scores, -jnp.inf)
        top = jnp.max(scores, axis=1, keepdims=True)
        weight = jnp.exp(scores - top)
        total = jnp.sum(weight, axis=1, keepdims=True)
        mixed_ref[0, j] = jnp.dot(weight.astype(BF16), v_ref[0, :, lanes], preferred_element_type=F32)
        top_ref[0, j] = jnp.broadcast_to(top, top_ref.shape[2:])
        total_ref[0, j] = jnp.broadcast_to(total, total_ref.shape[2:])


def attend_cache(queries, cache_keys, cache_values, lengths):
    count, steps, width = queries.shape
    slots = cache_keys.shape[1]
    groups = cache_keys.shape[2] // HD
    share = width // cache_keys.shape[2]
    state = jax.ShapeDtypeStruct((count, groups, share * steps, HD), F32)
    state_spec = pl.BlockSpec((1, groups, share * steps, HD), lambda r, n: (r, 0, 0, 0))
    cache_spec = pl.BlockSpec((1, slots, groups * HD), lambda r, n: (r, 0, 0))
    return pl.pallas_call(
        lambda *refs: cache_kernel(*refs, groups=groups, share=share),
        out_shape=(state, state, state),
        grid_spec=pltpu.PrefetchScalarGridSpec(
            num_scalar_prefetch=1,
            grid=(count,),
            in_specs=[
                pl.BlockSpec((1, steps, width), lambda r, n: (r, 0, 0)),
                cache_spec,
                cache_spec,
            ],
            out_specs=[state_spec, state_spec, state_spec],
        ),
        cost_estimate=pl.CostEstimate(
            flops=4 * count * groups * share * steps * slots * HD,
            bytes_accessed=4 * count * slots * groups * HD,
            transcendentals=count * groups * share * steps * slots,
        ),
        name="cache_attention",
    )(lengths, queries, cache_keys, cache_values)


def fresh_kernel(
    same_ref, other_ref, cos_ref, sin_ref, q_ref, v_ref, mixed_ref, top_ref, total_ref, keys_ref, out_ref
):
    count, steps, width = q_ref.shape
    groups = v_ref.shape[2] // HD
    share = width // v_ref.shape[2]
    for r in range(count):
        lines = slice(r * steps, (r + 1) * steps)
        for j in range(groups):
            lanes = slice(j * HD, (j + 1) * HD)
            heads = slice(j * share * HD, (j + 1) * share * HD)
            raw = same_ref[lines, lanes] + other_ref[lines, lanes]
            keys = raw * cos_ref[lines, :] + pltpu.roll(raw, HD // 2, 1) * sin_ref[lines, :]
            keys = keys.astype(BF16)
            keys_ref[r, :, lanes] = keys
            query = stacked(q_ref[r, :, heads], share).astype(BF16)
            scores = lax.dot_general(
                query, keys, (((1,), (1,)), ((), ())), preferred_element_type=F32
            ) * (1.0 / math.sqrt(HD))
            step = lax.broadcasted_iota(jnp.int32, scores.shape, 0) % steps
            seen = lax.broadcasted_iota(jnp.int32, scores.shape, 1) <= step
            scores = jnp.where(seen, scores, -jnp.inf)
            top = top_ref[r, j]
            high = jnp.maximum(top, jnp.max(scores, axis=1, keepdims=True))
            old = jnp.exp(top - high)
            weight = jnp.exp(scores - high[:, :1])
            whole = total_ref[r, j] * old + jnp.sum(weight, axis=1, keepdims=True)
            fresh = jnp.dot(weight.astype(BF16), v_ref[r, :, lanes], preferred_element_type=F32)
            context = (mixed_ref[r, j] * old + fresh) / whole
            flat = [context[h * steps : (h + 1) * steps] for h in range(share)]
            out_ref[r, :, heads] = jnp.concatenate(flat, axis=1).astype(BF16)


def attend_fresh(same, other, cosine, sine, queries, new_values, mixed, top, total):
    return pl.pallas_call(
        fresh_kernel,
        out_shape=(
            jax.ShapeDtypeStruct(new_values.shape, BF16),
            jax.ShapeDtypeStruct(queries.shape, BF16),
        ),
        name="fresh_attention",
    )(same, other, cosine, sine, queries, new_values, mixed, top, total)


def input_kernel(place, m_ref, w_ref, *refs):
    weight = jnp.concatenate([w_ref[0, b, 0] for b in range(w_ref.shape[1])], axis=1)
    refs[-1][...] = lax.dot_general(
        m_ref[...], weight, (((1,), (1,)), ((), ())), preferred_element_type=F32
    ).astype(BF16)


def input_grad(masked, weight, place, number, out, wide):
    pieces, blocks, two, rows, cols = weight.shape
    count = masked.shape[0]
    more = [] if out is None else [out]
    return pl.pallas_call(
        input_kernel,
        out_shape=jax.ShapeDtypeStruct((count, wide), BF16),
        grid_spec=pltpu.PrefetchScalarGridSpec(
            num_scalar_prefetch=1,
            grid=(pieces, two),
            in_specs=[
                pl.BlockSpec((count, blocks * cols), lambda q, j, n: (0, 0)),
                pl.BlockSpec((1, blocks, 1, rows, cols), lambda q, j, n: (q, 0, j, 0, 0)),
            ]
            + [pl.BlockSpec(memory_space=pl.ANY) for _ in more],
            out_specs=pl.BlockSpec(
                (count, rows),
                lambda q, j, n: (0, j * NX * NY + (q ^ n[0]) * NY + n[number]),
            ),
        ),
        input_output_aliases={3: 0} if more else {},
        cost_estimate=pl.CostEstimate(
            flops=2 * count * weight.size, bytes_accessed=2 * weight.size, transcendentals=0
        ),
        name="input_grad",
    )(place, masked, weight, *more)


def angles(lengths, steps):
    half = HD // 2
    freq = ROPE_BASE ** (-jnp.arange(half, dtype=F32) * (2.0 / HD))
    positions = lengths[:, None] + jnp.arange(steps, dtype=jnp.int32)[None, :]
    angle = positions.reshape(-1).astype(F32)[:, None] * freq
    cosine, sine = jnp.cos(angle), jnp.sin(angle)
    return jnp.concatenate([cosine, cosine], axis=1), jnp.concatenate([-sine, sine], axis=1)


def update_and_decode(
    tokens,
    cotangent,
    response_mask,
    key_weight,
    new_hidden,
    new_values,
    queries,
    cache_keys,
    cache_values,
    cache_lengths,
):
    z, xh, y = lax.axis_index("z"), lax.axis_index("xh"), lax.axis_index("y")
    xl, c = lax.axis_index("xl"), lax.axis_index("c")
    tp = xl * NC + c
    odd = z & 1
    wide = tokens.shape[1]
    cols = cotangent.shape[1]
    rows = key_weight.shape[0]
    requests, steps = new_hidden.shape[0], new_hidden.shape[1]
    lines = requests * steps

    masked = cotangent * response_mask[:, None].astype(BF16)
    masked_all = lax.all_gather(masked, TP, axis=1, tiled=True)

    hidden = new_hidden.reshape(lines, new_hidden.shape[2])
    hidden = lax.dynamic_slice_in_dim(hidden, tp * wide, wide, 1)
    hidden = hidden.reshape(lines, 2, NX * NY, rows).transpose(2, 1, 0, 3)
    hidden = lax.all_to_all(hidden, ("xh", "y"), 0, 0, tiled=True)
    hidden = hidden.transpose(1, 0, 2, 3).reshape(1, 2, NX * NY * lines, rows)
    hidden = jnp.broadcast_to(hidden, (NZ // 2,) + hidden.shape[1:]).reshape(NZ, NX * NY * lines, rows)
    hidden = lax.all_to_all(hidden, "z", 0, 0, tiled=True)
    hidden = hidden.reshape(NZ, NX * NY, lines, rows).transpose(1, 0, 2, 3).reshape(-1, rows)

    own_weight = swap_owner(key_weight)
    old = jnp.broadcast_to(own_weight, (NZ, rows, cols))
    old = lax.all_to_all(old, "z", 0, 0, tiled=True)
    old = old.reshape(NL * NC, 2, rows, cols)
    other = shift(old, "xh", NX, 1)
    old = jnp.stack([old, other])
    up = shift(old, "y", NY, 1)
    down = shift(old, "y", NY, -1)
    far = shift(up, "y", NY, 1)

    def term(k):
        left = lax.dynamic_slice_in_dim(tokens, (k & 1) * (wide // 2), wide // 2, 1)
        right = lax.dynamic_slice_in_dim(masked_all, (k >> 1) * cols, cols, 1)
        return lax.dot_general(left, right, (((0,), (0,)), ((), ())), preferred_element_type=F32)

    part = ring_sum(term, "z", NZ, z).reshape(NX, NY, rows, cols)
    part = part.astype(BF16).reshape(NX * NY, rows, cols)
    part = lax.all_to_all(part, ("xh", "y"), 0, 0, tiled=True)
    grad = jnp.sum(part.astype(F32), axis=0)

    scale = 1.0 / math.sqrt(D * tokens.shape[0] * NZ * NX * NY)
    own_weight = (own_weight.astype(F32) - grad * scale).astype(BF16)

    raw = jnp.dot(hidden, own_weight, preferred_element_type=F32).astype(BF16)
    raw = raw.reshape(NX * NY, NZ * lines, cols)
    raw = lax.all_to_all(raw, ("xh", "y"), 0, 0, tiled=True)
    raw = jnp.sum(raw.astype(F32), axis=0).reshape(NL, NC, 2, lines, cols)
    other = shift(pick(raw, 1 - c, 1), "c", NC, 1)
    raw = pick(raw, c, 1) + other
    other = shift(pick(raw, 1 - xl, 0), "xl", NL, 1)
    raw = pick(raw, xl, 0) + other
    same = swap_owner(pick(raw, odd, 0))
    other = swap_owner(pick(raw, 1 - odd, 0), 1)

    learner_weight = swap_owner(own_weight)

    state = attend_cache(queries, cache_keys, cache_values, cache_lengths)
    cosine, sine = angles(cache_lengths, steps)
    new_keys, context = attend_fresh(same, other, cosine, sine, queries, new_values, *state)

    place = jnp.stack([xh, y, (y - 1) & (NY - 1), (y + 1) & (NY - 1), y ^ 2]).astype(jnp.int32)
    grad_inputs = None
    for number, weight in enumerate((old, up, down, far)):
        grad_inputs = input_grad(masked_all, weight, place, number + 1, grad_inputs, wide)
    return (grad_inputs, learner_weight, new_keys, context)


def solution(mesh):
    split = Mesh(mesh.devices.reshape(NZ, NX, NY, NL, NC), ("z", "xh", "y", "xl", "c"))
    placed = (
        P(FSDP, TP),
        P(FSDP, TP),
        P(FSDP),
        P(FSDP, TP),
        P(FSDP, None, None),
        P(FSDP, None, TP),
        P(FSDP, None, TP),
        P(FSDP, None, TP),
        P(FSDP, None, TP),
        P(FSDP),
    )
    return jax.shard_map(
        update_and_decode,
        mesh=split,
        in_specs=placed,
        out_specs=(P(FSDP, TP), P(FSDP, TP), P(FSDP, None, TP), P(FSDP, None, TP)),
        check_vma=False,
    )
```

```python
import math

import jax
import jax.numpy as jnp
from jax import lax
from jax.experimental import pallas as pl
from jax.experimental.pallas import tpu as pltpu
from jax.sharding import Mesh, PartitionSpec as P


D = 8192
HD = 128
NZ, NX, NY, NL, NC = 8, 2, 4, 2, 2
FSDP = ("zh", "zl", "xh", "y")
Z = ("zh", "zl")
TP = ("xl", "c")
F32 = jnp.float32
BF16 = jnp.bfloat16

ROPE_BASE = 1000000.0


def shift(x, axis, size, step):
    return lax.ppermute(x, axis, [(i, (i + step) % size) for i in range(size)])


def swap_owner(x):
    pairs = []
    for z in range(NZ):
        for t in range(NL * NC):
            pairs.append((z * 4 + t, (2 * t + z % 2) * 4 + z // 2))
    return lax.ppermute(x, Z + TP, pairs)


def ring_sum(term, axis, size, me):
    last = size // 2
    whole = term((me + last) & (size - 1)).astype(BF16)
    half = whole.shape[0] // 2
    up, down = whole[:half], whole[half:]

    def low(x):
        return jnp.pad(x, [(0, half), (0, 0)])

    def high(x):
        return jnp.pad(x, [(half, 0), (0, 0)])

    for hop in range(last, 0, -1):
        if hop < last:
            plus, minus = term((me + hop) & (size - 1)), term((me - hop) & (size - 1))
            up, down = up.astype(F32), down.astype(F32)
            if hop == last - 1:
                up, down = low(up), high(down)
            up, down = (plus + up).astype(BF16), (minus + down).astype(BF16)
        up = shift(up, axis, size, 1)
        down = shift(down, axis, size, -1)
    return term(me) + up.astype(F32) + down.astype(F32)


def stacked(flat, share):
    wide = flat.astype(F32)
    return jnp.concatenate([wide[:, h * HD : (h + 1) * HD] for h in range(share)], axis=0)


def cache_kernel(lengths, q_ref, k_ref, v_ref, mixed_ref, top_ref, total_ref, *, groups, share):
    valid = lengths[pl.program_id(0)]
    for j in range(groups):
        lanes = slice(j * HD, (j + 1) * HD)
        query = stacked(q_ref[0, :, j * share * HD : (j + 1) * share * HD], share).astype(BF16)
        scores = lax.dot_general(
            query, k_ref[0, :, lanes], (((1,), (1,)), ((), ())), preferred_element_type=F32
        ) * (1.0 / math.sqrt(HD))
        slot = lax.broadcasted_iota(jnp.int32, scores.shape, 1)
        scores = jnp.where(slot < valid, scores, -jnp.inf)
        top = jnp.max(scores, axis=1, keepdims=True)
        weight = jnp.exp(scores - top)
        total = jnp.sum(weight, axis=1, keepdims=True)
        mixed_ref[0, j] = jnp.dot(weight.astype(BF16), v_ref[0, :, lanes], preferred_element_type=F32)
        top_ref[0, j] = jnp.broadcast_to(top, top_ref.shape[2:])
        total_ref[0, j] = jnp.broadcast_to(total, total_ref.shape[2:])


def attend_cache(queries, cache_keys, cache_values, lengths):
    count, steps, width = queries.shape
    slots = cache_keys.shape[1]
    groups = cache_keys.shape[2] // HD
    share = width // cache_keys.shape[2]
    state = jax.ShapeDtypeStruct((count, groups, share * steps, HD), F32)
    state_spec = pl.BlockSpec((1, groups, share * steps, HD), lambda r, n: (r, 0, 0, 0))
    cache_spec = pl.BlockSpec((1, slots, groups * HD), lambda r, n: (r, 0, 0))
    return pl.pallas_call(
        lambda *refs: cache_kernel(*refs, groups=groups, share=share),
        out_shape=(state, state, state),
        grid_spec=pltpu.PrefetchScalarGridSpec(
            num_scalar_prefetch=1,
            grid=(count,),
            in_specs=[
                pl.BlockSpec((1, steps, width), lambda r, n: (r, 0, 0)),
                cache_spec,
                cache_spec,
            ],
            out_specs=[state_spec, state_spec, state_spec],
        ),
        cost_estimate=pl.CostEstimate(
            flops=4 * count * groups * share * steps * slots * HD,
            bytes_accessed=4 * count * slots * groups * HD,
            transcendentals=count * groups * share * steps * slots,
        ),
        name="cache_attention",
    )(lengths, queries, cache_keys, cache_values)


def fresh_kernel(
    raw_ref, cos_ref, sin_ref, q_ref, v_ref, mixed_ref, top_ref, total_ref, keys_ref, out_ref
):
    count, steps, width = q_ref.shape
    groups = v_ref.shape[2] // HD
    share = width // v_ref.shape[2]
    for r in range(count):
        lines = slice(r * steps, (r + 1) * steps)
        for j in range(groups):
            lanes = slice(j * HD, (j + 1) * HD)
            heads = slice(j * share * HD, (j + 1) * share * HD)
            raw = raw_ref[lines, lanes]
            keys = raw * cos_ref[lines, :] + pltpu.roll(raw, HD // 2, 1) * sin_ref[lines, :]
            keys = keys.astype(BF16)
            keys_ref[r, :, lanes] = keys
            query = stacked(q_ref[r, :, heads], share).astype(BF16)
            scores = lax.dot_general(
                query, keys, (((1,), (1,)), ((), ())), preferred_element_type=F32
            ) * (1.0 / math.sqrt(HD))
            step = lax.broadcasted_iota(jnp.int32, scores.shape, 0) % steps
            seen = lax.broadcasted_iota(jnp.int32, scores.shape, 1) <= step
            scores = jnp.where(seen, scores, -jnp.inf)
            top = top_ref[r, j]
            high = jnp.maximum(top, jnp.max(scores, axis=1, keepdims=True))
            old = jnp.exp(top - high)
            weight = jnp.exp(scores - high[:, :1])
            whole = total_ref[r, j] * old + jnp.sum(weight, axis=1, keepdims=True)
            fresh = jnp.dot(weight.astype(BF16), v_ref[r, :, lanes], preferred_element_type=F32)
            context = (mixed_ref[r, j] * old + fresh) / whole
            flat = [context[h * steps : (h + 1) * steps] for h in range(share)]
            out_ref[r, :, heads] = jnp.concatenate(flat, axis=1).astype(BF16)


def attend_fresh(raw, cosine, sine, queries, new_values, mixed, top, total):
    return pl.pallas_call(
        fresh_kernel,
        out_shape=(
            jax.ShapeDtypeStruct(new_values.shape, BF16),
            jax.ShapeDtypeStruct(queries.shape, BF16),
        ),
        name="fresh_attention",
    )(raw, cosine, sine, queries, new_values, mixed, top, total)


def input_kernel(place, m_ref, w_ref, *refs, number):
    out_ref, stage, sems = refs[-3:]
    pieces, blocks, two, rows, cols = w_ref.shape
    copies = []
    for q in range(pieces):
        weight = jnp.concatenate(
            [w_ref[q, b].reshape(two * rows, cols) for b in range(blocks)], axis=1
        )
        product = lax.dot_general(
            m_ref[...], weight, (((1,), (1,)), ((), ())), preferred_element_type=F32
        ).astype(BF16)
        for j in range(two):
            slot = q * two + j
            stage[slot] = product[:, j * rows : (j + 1) * rows]
            column = (j * NX * NY + (q ^ place[0]) * NY + place[number]) * rows
            copy = pltpu.make_async_copy(
                stage.at[slot], out_ref.at[:, pl.ds(pl.multiple_of(column, rows), rows)], sems.at[slot]
            )
            copy.start()
            copies.append(copy)
    for copy in copies:
        copy.wait()


def input_grad(masked, weight, place, number, out, wide):
    pieces, _, two, rows, _ = weight.shape
    count = masked.shape[0]
    more = [] if out is None else [out]
    return pl.pallas_call(
        lambda *refs: input_kernel(*refs, number=number),
        out_shape=jax.ShapeDtypeStruct((count, wide), BF16),
        in_specs=[
            pl.BlockSpec(memory_space=pltpu.SMEM),
            pl.BlockSpec(memory_space=pltpu.VMEM),
            pl.BlockSpec(memory_space=pltpu.VMEM),
        ]
        + [pl.BlockSpec(memory_space=pl.ANY) for _ in more],
        out_specs=pl.BlockSpec(memory_space=pl.ANY),
        scratch_shapes=[
            pltpu.VMEM((pieces * two, count, rows), BF16),
            pltpu.SemaphoreType.DMA((pieces * two,)),
        ],
        input_output_aliases={3: 0} if more else {},
        cost_estimate=pl.CostEstimate(
            flops=2 * count * weight.size, bytes_accessed=2 * weight.size, transcendentals=0
        ),
        name="input_grad",
    )(place, masked, weight, *more)


def angles(lengths, steps):
    half = HD // 2
    freq = ROPE_BASE ** (-jnp.arange(half, dtype=F32) * (2.0 / HD))
    positions = lengths[:, None] + jnp.arange(steps, dtype=jnp.int32)[None, :]
    angle = positions.reshape(-1).astype(F32)[:, None] * freq
    cosine, sine = jnp.cos(angle), jnp.sin(angle)
    return jnp.concatenate([cosine, cosine], axis=1), jnp.concatenate([-sine, sine], axis=1)


def update_and_decode(
    tokens,
    cotangent,
    response_mask,
    key_weight,
    new_hidden,
    new_values,
    queries,
    cache_keys,
    cache_values,
    cache_lengths,
):
    z, xh, y = lax.axis_index(Z), lax.axis_index("xh"), lax.axis_index("y")
    tp = lax.axis_index(TP)
    wide = tokens.shape[1]
    cols = cotangent.shape[1]
    rows = key_weight.shape[0]
    requests, steps = new_hidden.shape[0], new_hidden.shape[1]
    lines = requests * steps

    masked = cotangent * response_mask[:, None].astype(BF16)
    masked_all = lax.all_gather(masked, TP, axis=1, tiled=True)

    hidden = new_hidden.reshape(lines, new_hidden.shape[2])
    hidden = lax.dynamic_slice_in_dim(hidden, tp * wide, wide, 1)
    hidden = hidden.reshape(lines, 2, NX * NY, rows).transpose(2, 1, 0, 3)
    hidden = lax.all_to_all(hidden, ("xh", "y"), 0, 0, tiled=True)
    hidden = hidden.transpose(1, 0, 2, 3).reshape(1, 2, NX * NY * lines, rows)
    hidden = jnp.broadcast_to(hidden, (NZ // 2,) + hidden.shape[1:]).reshape(NZ, NX * NY * lines, rows)
    hidden = lax.all_to_all(hidden, Z, 0, 0, tiled=True)
    hidden = hidden.reshape(NZ, NX * NY, lines, rows).transpose(1, 0, 2, 3).reshape(-1, rows)

    own_weight = swap_owner(key_weight)
    old = jnp.broadcast_to(own_weight, (NZ, rows, cols))
    old = lax.all_to_all(old, Z, 0, 0, tiled=True)
    old = old.reshape(NL * NC, 2, rows, cols)
    other = shift(old, "xh", NX, 1)
    old = jnp.stack([old, other])
    up = shift(old, "y", NY, 1)
    down = shift(old, "y", NY, -1)
    far = shift(up, "y", NY, 1)

    def term(k):
        left = lax.dynamic_slice_in_dim(tokens, (k & 1) * (wide // 2), wide // 2, 1)
        right = lax.dynamic_slice_in_dim(masked_all, (k >> 1) * cols, cols, 1)
        return lax.dot_general(left, right, (((0,), (0,)), ((), ())), preferred_element_type=F32)

    part = ring_sum(term, Z, NZ, z).reshape(NX, NY, rows, cols)
    part = part.astype(BF16).reshape(NX * NY, rows, cols)
    part = lax.all_to_all(part, ("xh", "y"), 0, 0, tiled=True)
    grad = jnp.sum(part.astype(F32), axis=0)

    scale = 1.0 / math.sqrt(D * tokens.shape[0] * NZ * NX * NY)
    own_weight = (own_weight.astype(F32) - grad * scale).astype(BF16)

    raw = jnp.dot(hidden, own_weight, preferred_element_type=F32).astype(BF16)
    raw = raw.reshape(NX * NY, NZ * lines, cols)
    raw = lax.all_to_all(raw, ("xh", "y"), 0, 0, tiled=True)
    raw = jnp.sum(raw.astype(F32), axis=0).reshape(NL * NC, 2, lines, cols)
    raw = raw.transpose(1, 0, 2, 3).reshape(2 * NL * NC, lines, cols).astype(BF16)
    raw = lax.all_to_all(raw, ("zl",) + TP, 0, 0, tiled=True)
    raw = swap_owner(jnp.sum(raw.astype(F32), axis=0))

    learner_weight = swap_owner(own_weight)

    state = attend_cache(queries, cache_keys, cache_values, cache_lengths)
    cosine, sine = angles(cache_lengths, steps)
    new_keys, context = attend_fresh(raw, cosine, sine, queries, new_values, *state)

    place = jnp.stack([xh, y, (y - 1) & (NY - 1), (y + 1) & (NY - 1), y ^ 2]).astype(jnp.int32)
    grad_inputs = None
    for number, weight in enumerate((old, up, down, far)):
        grad_inputs = input_grad(masked_all, weight, place, number + 1, grad_inputs, wide)
    return (grad_inputs, learner_weight, new_keys, context)


def solution(mesh):
    split = Mesh(mesh.devices.reshape(NZ // 2, 2, NX, NY, NL, NC), ("zh", "zl", "xh", "y", "xl", "c"))
    placed = (
        P(FSDP, TP),
        P(FSDP, TP),
        P(FSDP),
        P(FSDP, TP),
        P(FSDP, None, None),
        P(FSDP, None, TP),
        P(FSDP, None, TP),
        P(FSDP, None, TP),
        P(FSDP, None, TP),
        P(FSDP),
    )
    return jax.shard_map(
        update_and_decode,
        mesh=split,
        in_specs=placed,
        out_specs=(P(FSDP, TP), P(FSDP, TP), P(FSDP, None, TP), P(FSDP, None, TP)),
        check_vma=False,
    )
```

```python
import math

import jax
import jax.numpy as jnp
from jax import lax
from jax.experimental import pallas as pl
from jax.experimental.pallas import tpu as pltpu
from jax.sharding import Mesh, PartitionSpec as P


D = 8192
HD = 128
NZ, NX, NY, NL, NC = 8, 2, 4, 2, 2
FSDP = ("z", "xh", "y")
TP = ("xl", "c")
F32 = jnp.float32
BF16 = jnp.bfloat16

ROPE_BASE = 1000000.0


def shift(x, axis, size, step):
    return lax.ppermute(x, axis, [(i, (i + step) % size) for i in range(size)])


def swap_owner(x, flip=0):
    pairs = []
    for z in range(NZ):
        for t in range(NL * NC):
            pairs.append((z * 4 + t, (2 * t + (z % 2 ^ flip)) * 4 + z // 2))
    return lax.ppermute(x, ("z", "xl", "c"), pairs)


def pick(x, index, axis):
    return lax.dynamic_index_in_dim(x, index, axis, keepdims=False)


def ring_sum(term, axis, size, me):
    last = size // 2
    whole = term((me + last) & (size - 1)).astype(BF16)
    half = whole.shape[0] // 2
    up, down = whole[:half], whole[half:]

    def low(x):
        return jnp.pad(x, [(0, half), (0, 0)])

    def high(x):
        return jnp.pad(x, [(half, 0), (0, 0)])

    for hop in range(last, 0, -1):
        if hop < last:
            plus, minus = term((me + hop) & (size - 1)), term((me - hop) & (size - 1))
            up, down = up.astype(F32), down.astype(F32)
            if hop == last - 1:
                up, down = low(up), high(down)
            up, down = (plus + up).astype(BF16), (minus + down).astype(BF16)
        up = shift(up, axis, size, 1)
        down = shift(down, axis, size, -1)
    return term(me) + up.astype(F32) + down.astype(F32)


def stacked(flat, share):
    wide = flat.astype(F32)
    return jnp.concatenate([wide[:, h * HD : (h + 1) * HD] for h in range(share)], axis=0)


def cache_kernel(lengths, q_ref, k_ref, v_ref, mixed_ref, top_ref, total_ref, *, groups, share):
    valid = lengths[pl.program_id(0)]
    for j in range(groups):
        lanes = slice(j * HD, (j + 1) * HD)
        query = stacked(q_ref[0, :, j * share * HD : (j + 1) * share * HD], share).astype(BF16)
        scores = lax.dot_general(
            query, k_ref[0, :, lanes], (((1,), (1,)), ((), ())), preferred_element_type=F32
        ) * (1.0 / math.sqrt(HD))
        slot = lax.broadcasted_iota(jnp.int32, scores.shape, 1)
        scores = jnp.where(slot < valid, scores, -jnp.inf)
        top = jnp.max(scores, axis=1, keepdims=True)
        weight = jnp.exp(scores - top)
        total = jnp.sum(weight, axis=1, keepdims=True)
        mixed_ref[0, j] = jnp.dot(weight.astype(BF16), v_ref[0, :, lanes], preferred_element_type=F32)
        top_ref[0, j] = jnp.broadcast_to(top, top_ref.shape[2:])
        total_ref[0, j] = jnp.broadcast_to(total, total_ref.shape[2:])


def attend_cache(queries, cache_keys, cache_values, lengths):
    count, steps, width = queries.shape
    slots = cache_keys.shape[1]
    groups = cache_keys.shape[2] // HD
    share = width // cache_keys.shape[2]
    state = jax.ShapeDtypeStruct((count, groups, share * steps, HD), F32)
    state_spec = pl.BlockSpec((1, groups, share * steps, HD), lambda r, n: (r, 0, 0, 0))
    cache_spec = pl.BlockSpec((1, slots, groups * HD), lambda r, n: (r, 0, 0))
    return pl.pallas_call(
        lambda *refs: cache_kernel(*refs, groups=groups, share=share),
        out_shape=(state, state, state),
        grid_spec=pltpu.PrefetchScalarGridSpec(
            num_scalar_prefetch=1,
            grid=(count,),
            in_specs=[
                pl.BlockSpec((1, steps, width), lambda r, n: (r, 0, 0)),
                cache_spec,
                cache_spec,
            ],
            out_specs=[state_spec, state_spec, state_spec],
        ),
        cost_estimate=pl.CostEstimate(
            flops=4 * count * groups * share * steps * slots * HD,
            bytes_accessed=4 * count * slots * groups * HD,
            transcendentals=count * groups * share * steps * slots,
        ),
        name="cache_attention",
    )(lengths, queries, cache_keys, cache_values)


def fresh_kernel(
    same_ref, other_ref, cos_ref, sin_ref, q_ref, v_ref, mixed_ref, top_ref, total_ref, keys_ref, out_ref
):
    count, steps, width = q_ref.shape
    groups = v_ref.shape[2] // HD
    share = width // v_ref.shape[2]
    for r in range(count):
        lines = slice(r * steps, (r + 1) * steps)
        for j in range(groups):
            lanes = slice(j * HD, (j + 1) * HD)
            heads = slice(j * share * HD, (j + 1) * share * HD)
            raw = same_ref[lines, lanes] + other_ref[lines, lanes]
            keys = raw * cos_ref[lines, :] + pltpu.roll(raw, HD // 2, 1) * sin_ref[lines, :]
            keys = keys.astype(BF16)
            keys_ref[r, :, lanes] = keys
            query = stacked(q_ref[r, :, heads], share).astype(BF16)
            scores = lax.dot_general(
                query, keys, (((1,), (1,)), ((), ())), preferred_element_type=F32
            ) * (1.0 / math.sqrt(HD))
            step = lax.broadcasted_iota(jnp.int32, scores.shape, 0) % steps
            seen = lax.broadcasted_iota(jnp.int32, scores.shape, 1) <= step
            scores = jnp.where(seen, scores, -jnp.inf)
            top = top_ref[r, j]
            high = jnp.maximum(top, jnp.max(scores, axis=1, keepdims=True))
            old = jnp.exp(top - high)
            weight = jnp.exp(scores - high[:, :1])
            whole = total_ref[r, j] * old + jnp.sum(weight, axis=1, keepdims=True)
            fresh = jnp.dot(weight.astype(BF16), v_ref[r, :, lanes], preferred_element_type=F32)
            context = (mixed_ref[r, j] * old + fresh) / whole
            flat = [context[h * steps : (h + 1) * steps] for h in range(share)]
            out_ref[r, :, heads] = jnp.concatenate(flat, axis=1).astype(BF16)


def attend_fresh(same, other, cosine, sine, queries, new_values, mixed, top, total):
    return pl.pallas_call(
        fresh_kernel,
        out_shape=(
            jax.ShapeDtypeStruct(new_values.shape, BF16),
            jax.ShapeDtypeStruct(queries.shape, BF16),
        ),
        name="fresh_attention",
    )(same, other, cosine, sine, queries, new_values, mixed, top, total)


def input_kernel(place, m_ref, w_ref, *refs, number):
    out_ref, stage, sems = refs[-3:]
    pieces, blocks, two, rows, cols = w_ref.shape
    copies = []
    for q in range(pieces):
        weight = jnp.concatenate(
            [w_ref[q, b].reshape(two * rows, cols) for b in range(blocks)], axis=1
        )
        product = lax.dot_general(
            m_ref[...], weight, (((1,), (1,)), ((), ())), preferred_element_type=F32
        ).astype(BF16)
        for j in range(two):
            slot = q * two + j
            stage[slot] = product[:, j * rows : (j + 1) * rows]
            column = (j * NX * NY + (q ^ place[0]) * NY + place[number]) * rows
            copy = pltpu.make_async_copy(
                stage.at[slot], out_ref.at[:, pl.ds(pl.multiple_of(column, rows), rows)], sems.at[slot]
            )
            copy.start()
            copies.append(copy)
    for copy in copies:
        copy.wait()


def input_grad(masked, weight, place, number, out, wide):
    pieces, _, two, rows, _ = weight.shape
    count = masked.shape[0]
    more = [] if out is None else [out]
    return pl.pallas_call(
        lambda *refs: input_kernel(*refs, number=number),
        out_shape=jax.ShapeDtypeStruct((count, wide), BF16),
        in_specs=[
            pl.BlockSpec(memory_space=pltpu.SMEM),
            pl.BlockSpec(memory_space=pltpu.VMEM),
            pl.BlockSpec(memory_space=pltpu.VMEM),
        ]
        + [pl.BlockSpec(memory_space=pl.ANY) for _ in more],
        out_specs=pl.BlockSpec(memory_space=pl.ANY),
        scratch_shapes=[
            pltpu.VMEM((pieces * two, count, rows), BF16),
            pltpu.SemaphoreType.DMA((pieces * two,)),
        ],
        input_output_aliases={3: 0} if more else {},
        cost_estimate=pl.CostEstimate(
            flops=2 * count * weight.size, bytes_accessed=2 * weight.size, transcendentals=0
        ),
        name="input_grad",
    )(place, masked, weight, *more)


def angles(lengths, steps):
    half = HD // 2
    freq = ROPE_BASE ** (-jnp.arange(half, dtype=F32) * (2.0 / HD))
    positions = lengths[:, None] + jnp.arange(steps, dtype=jnp.int32)[None, :]
    angle = positions.reshape(-1).astype(F32)[:, None] * freq
    cosine, sine = jnp.cos(angle), jnp.sin(angle)
    return jnp.concatenate([cosine, cosine], axis=1), jnp.concatenate([-sine, sine], axis=1)


def update_and_decode(
    tokens,
    cotangent,
    response_mask,
    key_weight,
    new_hidden,
    new_values,
    queries,
    cache_keys,
    cache_values,
    cache_lengths,
):
    z, xh, y = lax.axis_index("z"), lax.axis_index("xh"), lax.axis_index("y")
    xl, c = lax.axis_index("xl"), lax.axis_index("c")
    tp = xl * NC + c
    odd = z & 1
    wide = tokens.shape[1]
    cols = cotangent.shape[1]
    rows = key_weight.shape[0]
    requests, steps = new_hidden.shape[0], new_hidden.shape[1]
    lines = requests * steps

    masked = cotangent * response_mask[:, None].astype(BF16)
    masked_all = lax.all_gather(masked, TP, axis=1, tiled=True)

    hidden = new_hidden.reshape(lines, new_hidden.shape[2])
    hidden = lax.dynamic_slice_in_dim(hidden, tp * wide, wide, 1)
    hidden = hidden.reshape(lines, 2, NX * NY, rows).transpose(2, 1, 0, 3)
    hidden = lax.all_to_all(hidden, ("xh", "y"), 0, 0, tiled=True)
    hidden = hidden.transpose(1, 0, 2, 3).reshape(1, 2, NX * NY * lines, rows)
    hidden = jnp.broadcast_to(hidden, (NZ // 2,) + hidden.shape[1:]).reshape(NZ, NX * NY * lines, rows)
    hidden = lax.all_to_all(hidden, "z", 0, 0, tiled=True)
    hidden = hidden.reshape(NZ, NX * NY, lines, rows).transpose(1, 0, 2, 3).reshape(-1, rows)

    own_weight = swap_owner(key_weight)
    old = jnp.broadcast_to(own_weight, (NZ, rows, cols))
    old = lax.all_to_all(old, "z", 0, 0, tiled=True)
    old = old.reshape(NL * NC, 2, rows, cols)
    other = shift(old, "xh", NX, 1)
    old = jnp.stack([old, other])
    up = shift(old, "y", NY, 1)
    down = shift(old, "y", NY, -1)
    far = shift(up, "y", NY, 1)

    def term(k):
        left = lax.dynamic_slice_in_dim(tokens, (k & 1) * (wide // 2), wide // 2, 1)
        right = lax.dynamic_slice_in_dim(masked_all, (k >> 1) * cols, cols, 1)
        return lax.dot_general(left, right, (((0,), (0,)), ((), ())), preferred_element_type=F32)

    part = ring_sum(term, "z", NZ, z).reshape(NX, NY, rows, cols)
    part = part.astype(BF16).reshape(NX * NY, rows, cols)
    part = lax.all_to_all(part, ("xh", "y"), 0, 0, tiled=True)
    grad = jnp.sum(part.astype(F32), axis=0)

    scale = 1.0 / math.sqrt(D * tokens.shape[0] * NZ * NX * NY)
    own_weight = (own_weight.astype(F32) - grad * scale).astype(BF16)

    raw = jnp.dot(hidden, own_weight, preferred_element_type=F32).astype(BF16)
    raw = raw.reshape(NX * NY, NZ * lines, cols)
    raw = lax.all_to_all(raw, ("xh", "y"), 0, 0, tiled=True)
    raw = jnp.sum(raw.astype(F32), axis=0).reshape(NL, NC, 2, lines, cols)
    other = shift(pick(raw, 1 - c, 1), "c", NC, 1)
    raw = pick(raw, c, 1) + other
    other = shift(pick(raw, 1 - xl, 0), "xl", NL, 1)
    raw = pick(raw, xl, 0) + other
    same = swap_owner(pick(raw, odd, 0))
    other = swap_owner(pick(raw, 1 - odd, 0), 1)

    learner_weight = swap_owner(own_weight)

    state = attend_cache(queries, cache_keys, cache_values, cache_lengths)
    cosine, sine = angles(cache_lengths, steps)
    new_keys, context = attend_fresh(same, other, cosine, sine, queries, new_values, *state)

    place = jnp.stack([xh, y, (y - 1) & (NY - 1), (y + 1) & (NY - 1), y ^ 2]).astype(jnp.int32)
    grad_inputs = None
    for number, weight in enumerate((old, up, down, far)):
        grad_inputs = input_grad(masked_all, weight, place, number + 1, grad_inputs, wide)
    return (grad_inputs, learner_weight, new_keys, context)


def solution(mesh):
    split = Mesh(mesh.devices.reshape(NZ, NX, NY, NL, NC), ("z", "xh", "y", "xl", "c"))
    placed = (
        P(FSDP, TP),
        P(FSDP, TP),
        P(FSDP),
        P(FSDP, TP),
        P(FSDP, None, None),
        P(FSDP, None, TP),
        P(FSDP, None, TP),
        P(FSDP, None, TP),
        P(FSDP, None, TP),
        P(FSDP),
    )
    return jax.shard_map(
        update_and_decode,
        mesh=split,
        in_specs=placed,
        out_specs=(P(FSDP, TP), P(FSDP, TP), P(FSDP, None, TP), P(FSDP, None, TP)),
        check_vma=False,
    )
```
